32 devices in a mesh: tile: 8 (over y, x, core), blk: 4 (over z).
Axes of the slice: x: 2, y: 2, z: 4, core: 2. Of those that a mesh axis runs over, the one named last changes fastest.
Arguments:
- model_anoms: bfloat16 [24576, 256], P(('tile', 'blk')), may hold values from -6 to 6
- block_map: int32 [32, 768], P(('tile', 'blk')), may hold values from 0 to 767, each once within a row
- vectors: bfloat16 [2, 24576], P(None, ('tile', 'blk')), may hold values from -6 to 6
- positions: bfloat16 [3, 24576], P(None, ('tile', 'blk')), may hold values from 0 to 3
- pattern: int32 [192, 24], P(('tile', 'blk')), may hold values from 0 to 1, as said below
- pair_scale: float32 [192, 24], P(('tile', 'blk')), may hold values from 0.3 to 1
Outputs:
- applied: float32 [2, 24576], P(None, ('tile', 'blk'))
The draws below stay inside these ranges and needn't reach their ends.
Inputs may be any that keep to these rules, and one draw needn't show every extreme that they name: pattern is 1 on each block with itself and symmetric within a group of 24 blocks.
All inputs are finite; a program needn't handle non-finite values.
Results may differ from the reference program's by a relative error of at most 0.0003.
Values may be sent and summed in bfloat16 or wider, within the bound.
A program may use at most 64 MiB of HBM per device.

```python
import math
import jax
import jax.numpy as jnp
from jax import lax

M = 256
BLOCK = 128
BD = 6
PTS_DEV = 768
GROUP_BLOCKS = 24
BLOCKS = 192
TOTAL = 24576
N_TILE = 8
N_BLK = 4
DEVICES = 32


def draw_pattern(key, part):
    radii = jax.random.randint(key, (BLOCKS,), 0, GROUP_BLOCKS // 2 + 1)
    radii = radii.at[0].set(0).at[2].set(0).at[1].set(GROUP_BLOCKS // 2)
    rows = jnp.arange(BLOCKS)
    cols = jnp.arange(GROUP_BLOCKS)
    base = rows // GROUP_BLOCKS * GROUP_BLOCKS
    col_radii = radii[base[:, None] + cols[None, :]]
    spacing = jnp.abs(rows[:, None] % GROUP_BLOCKS - cols[None, :])
    spacing = jnp.minimum(spacing, GROUP_BLOCKS - spacing)
    return jnp.where(spacing <= jnp.maximum(radii[:, None], col_radii), 1, 0).astype(jnp.int32)


def block_levels(stream_key, dims, cuts, smallest, largest):
    factor_of, own = 1.0, jax.random.fold_in(stream_key, 6)
    for position, shards_of in cuts:
        heights = jnp.exp(jax.random.uniform(jax.random.fold_in(own, position), (shards_of,), jnp.float32, smallest / len(cuts), largest / len(cuts)))
        factor_of = factor_of * jnp.repeat(heights, dims[position] // shards_of).reshape([-1 if axis == position else 1 for axis in range(len(dims))])
    return factor_of


def normal_values(key, extent, spread, reach, shards=(), kind=jnp.bfloat16):
    array = jax.random.normal(key, extent, jnp.float32) * spread
    if len(shards) > 0:
        array = block_levels(key, extent, shards, -0.22, 0.18) * array
    return jnp.clip(array, min=-reach, max=reach).astype(kind)


def setup_inputs(seed: int = 0) -> dict:
    streams_of = jax.random.split(jax.random.key(seed), 7)
    model_anoms = normal_values(streams_of[0], (TOTAL, M), 1.0, 6.0, ((0, 32),))
    block_map = jax.vmap(lambda own: jax.random.permutation(own, PTS_DEV))(jax.random.split(streams_of[1], DEVICES)).reshape((DEVICES, PTS_DEV)).astype(jnp.int32)
    vectors = normal_values(streams_of[2], (2, TOTAL), 1.0, 6.0, ((1, 32),))
    positions = jnp.clip(3.0 * jax.random.uniform(streams_of[3], (3, TOTAL), jnp.float32) ** block_levels(streams_of[3], (3, TOTAL), ((1, 32),), -0.2, 0.2), 0.0, 3.0).astype(jnp.bfloat16)
    pattern = draw_pattern(jax.random.fold_in(streams_of[6], 71), 0)
    pair_scale = jnp.clip(jnp.exp(math.log(1.0) - 1.2039728 * jax.random.uniform(streams_of[5], (BLOCKS, GROUP_BLOCKS), jnp.float32) ** block_levels(streams_of[5], (BLOCKS, GROUP_BLOCKS), ((0, 32),), -0.2, 0.2)), 0.3, 1.0)
    return {"model_anoms": model_anoms, "block_map": block_map, "vectors": vectors, "positions": positions, "pattern": pattern, "pair_scale": pair_scale}


def gaspari_cohn(own_pos, other_pos):
    dx = own_pos[0][:, None] - other_pos[0][None, :]
    dy = own_pos[1][:, None] - other_pos[1][None, :]
    dz = own_pos[2][:, None] - other_pos[2][None, :]
    dist = jnp.sqrt(dx * dx + dy * dy + dz * dz)
    inner = (((-0.25 * dist + 0.5) * dist + 0.625) * dist - 5.0 / 3.0) * dist * dist + 1.0
    outer = ((((dist / 12.0 - 0.5) * dist + 0.625) * dist + 5.0 / 3.0) * dist - 5.0) * dist + 4.0 - 2.0 / (3.0 * jnp.maximum(dist, 1.0))
    return jnp.where(dist <= 1.0, inner, jnp.where(dist <= 2.0, outer, 0.0))

def reference(model_anoms, block_map, vectors, positions, pattern, pair_scale):
    piece = PTS_DEV // N_TILE
    tiles = model_anoms.reshape(N_TILE, N_BLK, N_TILE, piece, M)
    received = jnp.transpose(tiles, (2, 1, 0, 3, 4)).reshape(DEVICES, PTS_DEV, M)
    anoms = jnp.take_along_axis(received, block_map.astype(jnp.int32)[:, :, None], axis=1)
    group_pts = N_BLK * PTS_DEV
    groups = anoms.reshape(N_TILE, group_pts, M)
    pos_f = positions.astype(jnp.float32)
    group_pos = jnp.transpose(pos_f.reshape(3, N_TILE, group_pts), (1, 0, 2))
    row_pos = jnp.transpose(pos_f.reshape(3, DEVICES, PTS_DEV), (1, 0, 2))
    group_vecs = jnp.transpose(vectors.astype(jnp.float32).reshape(2, N_TILE, group_pts), (1, 0, 2))
    links = (pattern.astype(jnp.float32) * pair_scale).reshape(DEVICES, BD, BD * N_BLK)
    owners = (jnp.arange(DEVICES) // N_BLK).astype(jnp.int32)

    def one_device(item):
        rows_anoms, rows_pos, rows_w, owner = item
        g_anoms = groups[owner]
        g_pos = group_pos[owner]
        g_v = group_vecs[owner]
        cov = lax.dot_general(rows_anoms, g_anoms, (((1,), (1,)), ((), ())), preferred_element_type=jnp.float32)
        kern = gaspari_cohn(rows_pos, g_pos)
        wide = jnp.repeat(jnp.repeat(rows_w, BLOCK, 0), BLOCK, 1)
        taper = cov * kern * wide / (M - 1)
        return lax.dot_general(g_v, taper, (((1,), (1,)), ((), ())), precision=lax.Precision.HIGHEST)
    result = lax.map(one_device, (anoms, row_pos, links, owners))
    return jnp.transpose(result, (1, 0, 2)).reshape(2, TOTAL)
```

```python
import functools

import jax
import jax.numpy as jnp
from jax import lax
from jax.experimental import pallas as pl
from jax.experimental.pallas import tpu as pltpu
from jax.sharding import PartitionSpec as P

BLOCK = 128
F32, BF16 = jnp.float32, jnp.bfloat16
MESH = pl.DeviceIdType.MESH
NT = (((1,), (1,)), ((), ()))
TN = (((0,), (0,)), ((), ()))
NN = (((1,), (0,)), ((), ()))


def dot(a, b, dims):
    return lax.dot_general(a, b, dims, preferred_element_type=F32)


def parts(x):
    high = x.astype(BF16).astype(F32)
    rest = x - high
    mid = rest.astype(BF16).astype(F32)
    return high, mid, rest - mid


def stacked(rows, width):
    at = lax.broadcasted_iota(jnp.int32, (16, width), 0)
    out = jnp.zeros((16, width), F32)
    for i, row in enumerate(rows):
        out = jnp.where(at == i, row, out)
    return out


def squared_length(x, y, z):
    return x * x + y * y + z * z


def gaspari_cohn(squared):
    squared = jnp.maximum(squared, 1e-20)
    inverse = lax.rsqrt(squared)
    r = squared * inverse
    t = jnp.maximum(2.0 - r, 0.0)
    t = t * t
    outer = (t * t) * (r * (1.0 / 12.0) + (1.0 / 6.0) - inverse * (1.0 / 24.0))
    inner = (((-0.25 * r + 0.5) * r + 0.625) * r - 5.0 / 3.0) * squared + 1.0
    return jnp.where(squared <= 1.0, inner, outer)


def kernel(n, tiles, blocks, exchange, anoms_ref, side_ref, back_ref, own_w_ref, out_ref,
           buf, sides, backs, one_hot, own_hot, own, p_aug, q_aug, v_col, w_row, acc,
           gave, got, a_send, a_recv, z_send, z_recv, s_send, s_recv, g_send, g_recv, local):
    tile, place = lax.axis_index("tile"), lax.axis_index("blk")
    half = n // 2
    pieces, piece, members = buf.shape[1:]
    rows = pieces * piece
    flip = lax.rem(tile, 2)

    def mirrored(i):
        return i + flip * (n - 1 - 2 * i)

    u = mirrored(place)

    barrier = pltpu.get_barrier_semaphore()
    greeted = n - 1
    for k in range(1, n):
        pl.semaphore_signal(barrier, inc=1, device_id=(tile, lax.rem(place + k, n)), device_id_type=MESH)
    if exchange:
        greeted += tiles - 1
        for k in range(1, tiles):
            pl.semaphore_signal(barrier, inc=1, device_id=(lax.rem(tile + k, tiles), place), device_id_type=MESH)
    pl.semaphore_wait(barrier, greeted)

    def exchanged(k):
        peer = lax.rem(tile + k, tiles)
        slot = place + lax.rem(peer, 2) * (n - 1 - 2 * place)
        return pltpu.make_async_remote_copy(
            src_ref=anoms_ref.at[peer], dst_ref=buf.at[slot, tile], send_sem=a_send.at[k],
            recv_sem=a_recv.at[k], device_id=(peer, place), device_id_type=MESH)

    def moved(j, c, to):
        return pltpu.make_async_remote_copy(
            src_ref=buf.at[j, c], dst_ref=buf.at[j, c], send_sem=z_send.at[j, c],
            recv_sem=z_recv.at[j, c], device_id=(tile, mirrored(to)), device_id_type=MESH)

    def side_moved(j, to, which):
        ref = (sides, backs)[which]
        return pltpu.make_async_remote_copy(
            src_ref=ref.at[j], dst_ref=ref.at[j], send_sem=s_send.at[j, which],
            recv_sem=s_recv.at[j, which], device_id=(tile, mirrored(to)), device_id_type=MESH)

    def given(j, source):
        return pltpu.make_async_remote_copy(
            src_ref=gave.at[j], dst_ref=got.at[source], send_sem=g_send.at[j],
            recv_sem=g_recv.at[source], device_id=(tile, mirrored(j)), device_id_type=MESH)

    sends_right = u < half
    sends_left = u > half
    sends_own = u != half
    own_to = jnp.where(u < half, u + 1, jnp.maximum(u - 1, 0))

    if exchange:
        for k in range(1, tiles):
            exchanged(k).start()
        here = [pltpu.make_async_copy(anoms_ref.at[tile], buf.at[u, tile], local.at[0])]
    else:
        here = [pltpu.make_async_copy(anoms_ref, buf.at[u], local.at[0])]
    here.append(pltpu.make_async_copy(side_ref, sides.at[u], local.at[1]))
    here.append(pltpu.make_async_copy(back_ref, backs.at[u], local.at[2]))
    for copy in here:
        copy.start()
    for copy in here:
        copy.wait()

    @pl.when(sends_own)
    def _():
        side_moved(u, own_to, 0).start()
        side_moved(u, own_to, 1).start()

    def piece_at(k):
        return lax.rem(tile + pieces - k, pieces) if exchange else k

    for k in range(pieces):
        if exchange and k > 0:
            exchanged(k).wait_recv()

        @pl.when(sends_own)
        def _():
            moved(u, piece_at(k), own_to).start()

    def hot_of(j, ref):
        row = sides[j, 5:6, :].astype(jnp.int32)
        for c in range(0, rows, BLOCK):
            at = lax.broadcasted_iota(jnp.int32, (BLOCK, rows), 0) + c
            ref[c:c + BLOCK, :] = jnp.where(at == row, 1.0, 0.0).astype(BF16)

    def prepare(j, hot, back):
        side = sides[j]
        w = own_w_ref[mirrored(j)]
        values = list(parts(side[3:4] * w)) + list(parts(side[4:5] * w)) + [side]
        if back:
            table = backs[j, place]
            column = lax.broadcasted_iota(jnp.int32, (8, rows), 1) // BLOCK
            wide = jnp.zeros((8, rows), F32)
            for b in range(blocks):
                wide = jnp.where(column == b, table[:, b:b + 1], wide)
            values += list(parts(wide))
        if len(values) % 2:
            values.append(jnp.zeros((8, rows), F32))
        turned = dot(jnp.concatenate(values, axis=0).astype(BF16), hot[...], NT)
        lines = [turned[0:8] + turned[8:16] + turned[16:24], turned[24:32] + turned[32:40] + turned[40:48]]
        if back:
            lines.append(turned[56:64] + turned[64:72] + turned[72:80])
        for b in range(blocks):
            for i, line in enumerate(lines):
                w_row[b, i:i + 1, :] = line[b:b + 1]
        x, y, z = turned[48:49], turned[49:50], turned[50:51]
        q_aug[...] = stacked(
            [-2.0 * x, -2.0 * y, -2.0 * z, 1.0, 1.0, 1.0, *parts(squared_length(x, y, z))],
            rows).astype(BF16)

    chunk = 2 * BLOCK
    per_chunk = rows // chunk

    def pair(j, back):
        if back:
            gave[j] = jnp.zeros((8, rows), F32)

        def one(b, carry):
            start = pl.multiple_of(b * BLOCK, BLOCK)
            mine = own[pl.ds(start, BLOCK), :]
            mine_aug = p_aug[:, pl.ds(start, BLOCK)]
            theirs = buf[j].reshape(rows, members)
            sums = [jnp.zeros((BLOCK, BLOCK), F32)] * 2
            for c in range(per_chunk):
                cut = slice(c * chunk, (c + 1) * chunk)
                cov = dot(mine, theirs[cut], NT)
                kern = cov * gaspari_cohn(dot(mine_aug, q_aug[:, cut], TN))
                for v in range(2):
                    term = kern * w_row[b, v:v + 1, cut]
                    sums[v] = sums[v] + term[:, :BLOCK] + term[:, BLOCK:]
                    if back:
                        column = v_col[v, pl.ds(start, BLOCK), :]
                        for s in range(2):
                            lanes = slice(c * chunk + s * BLOCK, c * chunk + (s + 1) * BLOCK)
                            down = jnp.sum(kern[:, s * BLOCK:(s + 1) * BLOCK] * column, axis=0, keepdims=True)
                            gave[j, v:v + 1, lanes] += down * w_row[b, 2:3, lanes]
            for v in range(2):
                acc[v, pl.ds(start, BLOCK), :] += sums[v]
            return carry

        lax.fori_loop(0, blocks, one, 0)

    acc[...] = jnp.zeros_like(acc)
    hot_of(u, own_hot)
    own[...] = dot(own_hot[...], buf[u].reshape(rows, members), TN).astype(BF16)
    side = sides[u]
    x, y, z = side[0:1], side[1:2], side[2:3]
    p_aug[...] = stacked(
        [x, y, z, *parts(squared_length(x, y, z)), 1.0, 1.0, 1.0], rows).astype(BF16)
    both = stacked([side[3:4], side[4:5]], rows).astype(BF16)
    for v in range(2):
        pick = jnp.where(lax.broadcasted_iota(jnp.int32, (16, BLOCK), 0) == v, 1.0, 0.0).astype(BF16)
        v_col[v] = dot(both, pick, TN)
    prepare(u, own_hot, False)
    pair(u, False)

    from_left = jnp.minimum(u, half)

    def arrive(j, onward, to):
        side_moved(j, to, 0).wait_recv()
        side_moved(j, to, 1).wait_recv()

        @pl.when(onward)
        def _():
            side_moved(j, to, 0).start()
            side_moved(j, to, 1).start()

        for k in range(pieces):
            moved(j, piece_at(k), to).wait_recv()

            @pl.when(onward)
            def _():
                moved(j, piece_at(k), to).start()

    def work(j):
        hot_of(j, one_hot)
        prepare(j, one_hot, True)
        pair(j, True)
        given(j, u).start()

    def distance(d, carry):
        right = from_left - d
        left = u + d

        @pl.when(right >= 0)
        def _():
            arrive(right, u < n - 1, jnp.minimum(u + 1, n - 1))
            work(right)

        @pl.when((u >= half) & (left < n))
        def _():
            arrive(left, u > half, jnp.maximum(u - 1, 0))
            work(left)

        return carry

    lax.fori_loop(1, max(half, n - 1 - half) + 1, distance, 0)

    total = jnp.zeros((8, rows), F32)
    got_any = []
    for other in range(n):
        comes = ((u < half) & (other > u)) | ((u > half) & (other >= half) & (other < u))

        @pl.when(comes)
        def _():
            given(other, other).wait_recv()

        @pl.when(jnp.logical_not(comes))
        def _():
            got[other] = jnp.zeros((8, rows), F32)

        total = total + got[other]
    returned = jnp.concatenate([*parts(total), jnp.zeros((8, rows), F32)], axis=0).astype(BF16)
    turned = dot(returned, own_hot[...], NN)
    out = turned[0:8] + turned[8:16] + turned[16:24]
    ones = jnp.ones((8, BLOCK), F32)
    for v in range(2):
        line = lax.dot_general(ones, acc[v], NT, precision=lax.Precision.HIGHEST, preferred_element_type=F32)
        out_ref[v:v + 1, :] = out[v:v + 1] + line[0:1]

    if exchange:
        for k in range(1, tiles):
            exchanged(k).wait_send()
    for j in range(n):
        passes = ((j == u) & sends_own) | ((j < from_left) & (u < n - 1)) | ((j > u) & (u > half))

        @pl.when(passes)
        def _():
            side_moved(j, own_to, 0).wait_send()
            side_moved(j, own_to, 1).wait_send()
            for c in range(pieces):
                moved(j, c, own_to).wait_send()

        @pl.when((j < from_left) | ((j > u) & (u >= half)))
        def _():
            given(j, u).wait_send()


def on_device(n, tiles, model_anoms, block_map, vectors, positions, pattern, pair_scale):
    rows, members = model_anoms.shape
    blocks = rows // BLOCK
    exchange = rows % (16 * tiles) == 0
    if exchange:
        pieces = tiles
        anoms = model_anoms.reshape(pieces, rows // pieces, members)
    else:
        pieces = rows // BLOCK
        anoms = lax.all_to_all(model_anoms, "tile", split_axis=0, concat_axis=0, tiled=True)
        anoms = anoms.reshape(pieces, rows // pieces, members)
    side = jnp.concatenate([
        positions.astype(F32), vectors.astype(F32), block_map.astype(F32), jnp.zeros((2, rows), F32)], axis=0)
    links = (pattern.astype(F32) * pair_scale / (members - 1)).reshape(blocks, n, blocks)
    back = jnp.pad(jnp.transpose(links, (1, 2, 0)), ((0, 0), (0, 8 - blocks), (0, BLOCK - blocks)))
    own_w = jnp.pad(jnp.repeat(jnp.transpose(links, (1, 0, 2)), BLOCK, axis=2), ((0, 0), (0, 8 - blocks), (0, 0)))
    vmem = pl.BlockSpec(memory_space=pltpu.VMEM)
    dma = pltpu.SemaphoreType.DMA
    return pl.pallas_call(
        functools.partial(kernel, n, tiles, blocks, exchange),
        out_shape=jax.ShapeDtypeStruct((2, rows), F32),
        in_specs=[vmem] * 4,
        out_specs=vmem,
        scratch_shapes=[
            pltpu.VMEM((n, pieces, rows // pieces, members), BF16),
            pltpu.VMEM((n, 8, rows), F32),
            pltpu.VMEM((n, n, 8, BLOCK), F32),
            pltpu.VMEM((rows, rows), BF16),
            pltpu.VMEM((rows, rows), BF16),
            pltpu.VMEM((rows, members), BF16),
            pltpu.VMEM((16, rows), BF16),
            pltpu.VMEM((16, rows), BF16),
            pltpu.VMEM((2, rows, BLOCK), F32),
            pltpu.VMEM((blocks, 8, rows), F32),
            pltpu.VMEM((2, rows, BLOCK), F32),
            pltpu.VMEM((n, 8, rows), F32),
            pltpu.VMEM((n, 8, rows), F32),
            dma((tiles,)), dma((tiles,)),
            dma((n, pieces)), dma((n, pieces)),
            dma((n, 2)), dma((n, 2)),
            dma((n,)), dma((n,)),
            dma((3,)),
        ],
        compiler_params=pltpu.CompilerParams(
            collective_id=0, has_side_effects=True, vmem_limit_bytes=56 * 2**20),
    )(anoms, side, back, own_w)


def solution(mesh):
    shape = dict(mesh.shape)
    return jax.shard_map(
        functools.partial(on_device, shape["blk"], shape["tile"]),
        mesh=mesh,
        in_specs=(
            P(("tile", "blk"), None),
            P(("tile", "blk"), None),
            P(None, ("tile", "blk")),
            P(None, ("tile", "blk")),
            P(("tile", "blk"), None),
            P(("tile", "blk"), None),
        ),
        out_specs=P(None, ("tile", "blk")),
        check_vma=False,
    )
```

```python
import functools

import jax
import jax.numpy as jnp
from jax import lax
from jax.experimental import pallas as pl
from jax.experimental.pallas import tpu as pltpu
from jax.sharding import PartitionSpec as P

BLOCK = 128
F32, BF16 = jnp.float32, jnp.bfloat16
MESH = pl.DeviceIdType.MESH
NT = (((1,), (1,)), ((), ()))
TN = (((0,), (0,)), ((), ()))
NN = (((1,), (0,)), ((), ()))


def dot(a, b, dims):
    return lax.dot_general(a, b, dims, preferred_element_type=F32)


def parts(x):
    high = x.astype(BF16).astype(F32)
    rest = x - high
    mid = rest.astype(BF16).astype(F32)
    return high, mid, rest - mid


def stacked(rows, width, height=16):
    at = lax.broadcasted_iota(jnp.int32, (height, width), 0)
    out = jnp.zeros((height, width), F32)
    for i, row in enumerate(rows):
        out = jnp.where(at == i, row, out)
    return out


def squared_length(x, y, z):
    return x * x + y * y + z * z


def gaspari_cohn(squared):
    squared = jnp.maximum(squared, 1e-20)
    inverse = lax.rsqrt(squared)
    r = squared * inverse
    t = jnp.maximum(2.0 - r, 0.0)
    t = t * t
    outer = (t * t) * (r * (1.0 / 12.0) + (1.0 / 6.0) - inverse * (1.0 / 24.0))
    inner = (((-0.25 * r + 0.5) * r + 0.625) * r - 5.0 / 3.0) * squared + 1.0
    return jnp.where(squared <= 1.0, inner, outer)


def kernel(n, tiles, blocks, exchange, anoms_ref, *refs):
    small_refs, (out_ref, buf), slots = refs[:5], refs[5:7], refs[7:12]
    (one_hot, own_hot, own, p_aug, q_aug, v_col, w_row, acc,
     gave, got, a_send, a_recv, z_send, z_recv, s_send, s_recv, g_send, g_recv, local) = refs[12:]
    positions, vectors, maps, patterns, scales = slots
    tile, place = lax.axis_index("tile"), lax.axis_index("blk")
    half = n // 2
    pieces, piece, members = buf.shape[1:]
    rows = pieces * piece
    flip = lax.rem(tile, 2)

    def mirrored(i):
        return i + flip * (n - 1 - 2 * i)

    u = mirrored(place)

    barrier = pltpu.get_barrier_semaphore()
    greeted = n - 1
    for k in range(1, n):
        pl.semaphore_signal(barrier, inc=1, device_id=(tile, lax.rem(place + k, n)), device_id_type=MESH)
    if exchange:
        greeted += tiles - 1
        for k in range(1, tiles):
            pl.semaphore_signal(barrier, inc=1, device_id=(lax.rem(tile + k, tiles), place), device_id_type=MESH)
    pl.semaphore_wait(barrier, greeted)

    def exchanged(k):
        peer = lax.rem(tile + k, tiles)
        slot = place + lax.rem(peer, 2) * (n - 1 - 2 * place)
        return pltpu.make_async_remote_copy(
            src_ref=anoms_ref.at[peer], dst_ref=buf.at[slot, tile], send_sem=a_send.at[k],
            recv_sem=a_recv.at[k], device_id=(peer, place), device_id_type=MESH)

    def moved(j, c, to):
        return pltpu.make_async_remote_copy(
            src_ref=buf.at[j, c], dst_ref=buf.at[j, c], send_sem=z_send.at[j, c],
            recv_sem=z_recv.at[j, c], device_id=(tile, mirrored(to)), device_id_type=MESH)

    def side_moved(j, to, which):
        ref = slots[which]
        return pltpu.make_async_remote_copy(
            src_ref=ref.at[j], dst_ref=ref.at[j], send_sem=s_send.at[j, which],
            recv_sem=s_recv.at[j, which], device_id=(tile, mirrored(to)), device_id_type=MESH)

    def given(j, source):
        return pltpu.make_async_remote_copy(
            src_ref=gave.at[j], dst_ref=got.at[source], send_sem=g_send.at[j],
            recv_sem=g_recv.at[source], device_id=(tile, mirrored(j)), device_id_type=MESH)

    sends_right = u < half
    sends_left = u > half
    sends_own = u != half
    own_to = jnp.where(u < half, u + 1, jnp.maximum(u - 1, 0))

    if exchange:
        for k in range(1, tiles):
            exchanged(k).start()
        here = [pltpu.make_async_copy(anoms_ref.at[tile], buf.at[u, tile], local.at[0])]
    else:
        here = [pltpu.make_async_copy(anoms_ref, buf.at[u], local.at[0])]
    for i in range(5):
        here.append(pltpu.make_async_copy(small_refs[i], slots[i].at[u], local.at[i + 1]))
    for copy in here:
        copy.start()
    for copy in here:
        copy.wait()

    def small_start(j, to):
        for i in range(5):
            side_moved(j, to, i).start()

    @pl.when(sends_right)
    def _():
        small_start(u, own_to)

    def piece_at(k):
        return lax.rem(tile + pieces - k, pieces) if exchange else k

    for k in range(pieces):
        if exchange and k > 0:
            exchanged(k).wait_recv()

        @pl.when(sends_right)
        def _():
            moved(u, piece_at(k), own_to).start()

    def hot_of(j, ref):
        row = maps[j]
        for c in range(0, rows, BLOCK):
            at = lax.broadcasted_iota(jnp.int32, (BLOCK, rows), 0) + c
            ref[c:c + BLOCK, :] = jnp.where(at == row, 1.0, 0.0).astype(BF16)

    def link_parts(j):
        links = patterns[j].astype(F32) * scales[j] / (members - 1)
        if blocks % 8:
            links = jnp.concatenate([links, jnp.zeros((8 - blocks, n * blocks), F32)], axis=0)
        return jnp.concatenate(parts(links), axis=0).astype(BF16)

    def prepare(j, hot, back):
        where = positions[j].astype(F32)
        vecs = vectors[j].astype(F32)
        side = stacked([where[0:1], where[1:2], where[2:3]], rows, 8)
        columns = n * blocks
        block_of = lax.broadcasted_iota(jnp.int32, (columns, rows), 1) // BLOCK
        at = lax.broadcasted_iota(jnp.int32, (columns, rows), 0)
        spread = jnp.where(at == block_of + mirrored(j) * blocks, 1.0, 0.0).astype(BF16)
        w = dot(link_parts(u), spread, NN)
        w = w[0:8] + w[8:16] + w[16:24]
        values = list(parts(vecs[0:1] * w)) + list(parts(vecs[1:2] * w)) + [side]
        if back:
            take = jnp.where(
                lax.broadcasted_iota(jnp.int32, (columns, 8), 0)
                == lax.broadcasted_iota(jnp.int32, (columns, 8), 1) + place * blocks, 1.0, 0.0).astype(BF16)
            taken = dot(link_parts(j), take, NN)
            repeated = jnp.where(
                lax.broadcasted_iota(jnp.int32, (8, rows), 1) // BLOCK
                == lax.broadcasted_iota(jnp.int32, (8, rows), 0), 1.0, 0.0)
            for i in range(3):
                values.append(dot(taken[8 * i:8 * i + 8].astype(BF16), repeated.astype(BF16), TN))
        if len(values) % 2:
            values.append(jnp.zeros((8, rows), F32))
        turned = dot(jnp.concatenate(values, axis=0).astype(BF16), hot[...], NT)
        lines = [turned[0:8] + turned[8:16] + turned[16:24], turned[24:32] + turned[32:40] + turned[40:48]]
        if back:
            lines.append(turned[56:64] + turned[64:72] + turned[72:80])
        for b in range(blocks):
            for i, line in enumerate(lines):
                w_row[b, i:i + 1, :] = line[b:b + 1]
        x, y, z = turned[48:49], turned[49:50], turned[50:51]
        q_aug[...] = stacked(
            [-2.0 * x, -2.0 * y, -2.0 * z, 1.0, 1.0, 1.0, *parts(squared_length(x, y, z))],
            rows).astype(BF16)

    chunk = 2 * BLOCK
    per_chunk = rows // chunk

    def pair(j, back):
        if back:
            gave[j] = jnp.zeros((8, rows), F32)

        def one(b, carry):
            start = pl.multiple_of(b * BLOCK, BLOCK)
            mine = own[pl.ds(start, BLOCK), :]
            mine_aug = p_aug[:, pl.ds(start, BLOCK)]
            theirs = buf[j].reshape(rows, members)
            sums = [jnp.zeros((BLOCK, BLOCK), F32)] * 2
            for c in range(per_chunk):
                cut = slice(c * chunk, (c + 1) * chunk)
                cov = dot(mine, theirs[cut], NT)
                kern = cov * gaspari_cohn(dot(mine_aug, q_aug[:, cut], TN))
                for v in range(2):
                    term = kern * w_row[b, v:v + 1, cut]
                    sums[v] = sums[v] + term[:, :BLOCK] + term[:, BLOCK:]
                    if back:
                        column = v_col[v, pl.ds(start, BLOCK), :]
                        for s in range(2):
                            lanes = slice(c * chunk + s * BLOCK, c * chunk + (s + 1) * BLOCK)
                            down = jnp.sum(kern[:, s * BLOCK:(s + 1) * BLOCK] * column, axis=0, keepdims=True)
                            gave[j, v:v + 1, lanes] += down * w_row[b, 2:3, lanes]
            for v in range(2):
                acc[v, pl.ds(start, BLOCK), :] += sums[v]
            return carry

        lax.fori_loop(0, blocks, one, 0)

    acc[...] = jnp.zeros_like(acc)
    hot_of(u, own_hot)
    own[...] = dot(own_hot[...], buf[u].reshape(rows, members), TN).astype(BF16)
    where = positions[u].astype(F32)
    x, y, z = where[0:1], where[1:2], where[2:3]
    p_aug[...] = stacked(
        [x, y, z, *parts(squared_length(x, y, z)), 1.0, 1.0, 1.0], rows).astype(BF16)
    vecs = vectors[u].astype(F32)
    both = stacked([vecs[0:1], vecs[1:2]], rows).astype(BF16)
    for v in range(2):
        pick = jnp.where(lax.broadcasted_iota(jnp.int32, (16, BLOCK), 0) == v, 1.0, 0.0).astype(BF16)
        v_col[v] = dot(both, pick, TN)
    prepare(u, own_hot, False)
    pair(u, False)

    @pl.when(sends_left)
    def _():
        small_start(u, own_to)
        for k in range(pieces):
            moved(u, piece_at(k), own_to).start()

    from_left = jnp.minimum(u, half)

    def arrive(j, onward, to):
        for i in range(5):
            side_moved(j, to, i).wait_recv()

        @pl.when(onward)
        def _():
            small_start(j, to)

        for k in range(pieces):
            moved(j, piece_at(k), to).wait_recv()

            @pl.when(onward)
            def _():
                moved(j, piece_at(k), to).start()

    def work(j):
        hot_of(j, one_hot)
        prepare(j, one_hot, True)
        pair(j, True)
        given(j, u).start()

    def arrive_right_going(d):
        right = from_left - d

        @pl.when(right >= 0)
        def _():
            arrive(right, u < n - 1, jnp.minimum(u + 1, n - 1))

    def distance(d, carry):
        right = from_left - d
        left = u + d

        @pl.when(right >= 0)
        def _():
            work(right)

        arrive_right_going(d + 1)

        @pl.when((u >= half) & (left < n))
        def _():
            arrive(left, u > half, jnp.maximum(u - 1, 0))
            work(left)

        return carry

    arrive_right_going(1)
    lax.fori_loop(1, max(half, n - 1 - half) + 1, distance, 0)

    total = jnp.zeros((8, rows), F32)
    got_any = []
    for other in range(n):
        comes = ((u < half) & (other > u)) | ((u > half) & (other >= half) & (other < u))

        @pl.when(comes)
        def _():
            given(other, other).wait_recv()

        @pl.when(jnp.logical_not(comes))
        def _():
            got[other] = jnp.zeros((8, rows), F32)

        total = total + got[other]
    returned = jnp.concatenate([*parts(total), jnp.zeros((8, rows), F32)], axis=0).astype(BF16)
    turned = dot(returned, own_hot[...], NN)
    out = turned[0:8] + turned[8:16] + turned[16:24]
    ones = jnp.ones((8, BLOCK), F32)
    for v in range(2):
        line = lax.dot_general(ones, acc[v], NT, precision=lax.Precision.HIGHEST, preferred_element_type=F32)
        out_ref[v:v + 1, :] = out[v:v + 1] + line[0:1]

    if exchange:
        for k in range(1, tiles):
            exchanged(k).wait_send()
    for j in range(n):
        passes = ((j == u) & sends_own) | ((j < from_left) & (u < n - 1)) | ((j > u) & (u > half))

        @pl.when(passes)
        def _():
            for i in range(5):
                side_moved(j, own_to, i).wait_send()
            for c in range(pieces):
                moved(j, c, own_to).wait_send()

        @pl.when((j < from_left) | ((j > u) & (u >= half)))
        def _():
            given(j, u).wait_send()


def on_device(n, tiles, model_anoms, block_map, vectors, positions, pattern, pair_scale):
    rows, members = model_anoms.shape
    blocks = rows // BLOCK
    exchange = rows % (16 * tiles) == 0
    if exchange:
        pieces = tiles
        anoms = model_anoms.reshape(pieces, rows // pieces, members)
    else:
        pieces = rows // BLOCK
        anoms = lax.all_to_all(model_anoms, "tile", split_axis=0, concat_axis=0, tiled=True)
        anoms = anoms.reshape(pieces, rows // pieces, members)
    vmem = pl.BlockSpec(memory_space=pltpu.VMEM)
    dma = pltpu.SemaphoreType.DMA
    return pl.pallas_call(
        functools.partial(kernel, n, tiles, blocks, exchange),
        out_shape=jax.ShapeDtypeStruct((2, rows), F32),
        in_specs=[vmem] * 6,
        out_specs=vmem,
        scratch_shapes=[
            pltpu.VMEM((n, pieces, rows // pieces, members), BF16),
            pltpu.VMEM((n, 3, rows), BF16),
            pltpu.VMEM((n, 2, rows), BF16),
            pltpu.VMEM((n, 1, rows), jnp.int32),
            pltpu.VMEM((n, blocks, n * blocks), jnp.int32),
            pltpu.VMEM((n, blocks, n * blocks), F32),
            pltpu.VMEM((rows, rows), BF16),
            pltpu.VMEM((rows, rows), BF16),
            pltpu.VMEM((rows, members), BF16),
            pltpu.VMEM((16, rows), BF16),
            pltpu.VMEM((16, rows), BF16),
            pltpu.VMEM((2, rows, BLOCK), F32),
            pltpu.VMEM((blocks, 8, rows), F32),
            pltpu.VMEM((2, rows, BLOCK), F32),
            pltpu.VMEM((n, 8, rows), F32),
            pltpu.VMEM((n, 8, rows), F32),
            dma((tiles,)), dma((tiles,)),
            dma((n, pieces)), dma((n, pieces)),
            dma((n, 5)), dma((n, 5)),
            dma((n,)), dma((n,)),
            dma((6,)),
        ],
        compiler_params=pltpu.CompilerParams(
            collective_id=0, has_side_effects=True, vmem_limit_bytes=56 * 2**20),
    )(anoms, positions, vectors, block_map, pattern, pair_scale)


def solution(mesh):
    shape = dict(mesh.shape)
    return jax.shard_map(
        functools.partial(on_device, shape["blk"], shape["tile"]),
        mesh=mesh,
        in_specs=(
            P(("tile", "blk"), None),
            P(("tile", "blk"), None),
            P(None, ("tile", "blk")),
            P(None, ("tile", "blk")),
            P(("tile", "blk"), None),
            P(("tile", "blk"), None),
        ),
        out_specs=P(None, ("tile", "blk")),
        check_vma=False,
    )
```

```python
import functools

import jax
import jax.numpy as jnp
from jax import lax
from jax.experimental import pallas as pl
from jax.experimental.pallas import tpu as pltpu
from jax.sharding import PartitionSpec as P

BLOCK = 128
F32, BF16 = jnp.float32, jnp.bfloat16
MESH = pl.DeviceIdType.MESH
NT = (((1,), (1,)), ((), ()))
TN = (((0,), (0,)), ((), ()))
NN = (((1,), (0,)), ((), ()))


def dot(a, b, dims):
    return lax.dot_general(a, b, dims, preferred_element_type=F32)


def parts(x):
    high = x.astype(BF16).astype(F32)
    rest = x - high
    mid = rest.astype(BF16).astype(F32)
    return high, mid, rest - mid


def stacked(rows, width, height=16):
    at = lax.broadcasted_iota(jnp.int32, (height, width), 0)
    out = jnp.zeros((height, width), F32)
    for i, row in enumerate(rows):
        out = jnp.where(at == i, row, out)
    return out


def squared_length(x, y, z):
    return x * x + y * y + z * z


def gaspari_cohn(squared):
    squared = jnp.maximum(squared, 1e-20)
    inverse = lax.rsqrt(squared)
    r = squared * inverse
    t = jnp.maximum(2.0 - r, 0.0)
    t = t * t
    outer = (t * t) * (r * (1.0 / 12.0) + (1.0 / 6.0) - inverse * (1.0 / 24.0))
    inner = (((-0.25 * r + 0.5) * r + 0.625) * r - 5.0 / 3.0) * squared + 1.0
    return jnp.where(squared <= 1.0, inner, outer)


def kernel(n, tiles, blocks, exchange, anoms_ref, *refs):
    small_refs, (out_ref, buf), slots = refs[:5], refs[5:7], refs[7:12]
    (one_hot, own_hot, own, p_aug, q_aug, v_col, w_row, acc,
     gave, got, a_send, a_recv, z_send, z_recv, s_send, s_recv, g_send, g_recv, local) = refs[12:]
    positions, vectors, maps, patterns, scales = slots
    tile, place = lax.axis_index("tile"), lax.axis_index("blk")
    half = n // 2
    pieces, piece, members = buf.shape[1:]
    rows = pieces * piece
    flip = lax.rem(tile, 2)

    def mirrored(i):
        return i + flip * (n - 1 - 2 * i)

    u = mirrored(place)

    barrier = pltpu.get_barrier_semaphore()
    greeted = n - 1
    for k in range(1, n):
        pl.semaphore_signal(barrier, inc=1, device_id=(tile, lax.rem(place + k, n)), device_id_type=MESH)
    if exchange:
        greeted += tiles - 1
        for k in range(1, tiles):
            pl.semaphore_signal(barrier, inc=1, device_id=(lax.rem(tile + k, tiles), place), device_id_type=MESH)
    pl.semaphore_wait(barrier, greeted)

    def exchanged(k):
        peer = lax.rem(tile + k, tiles)
        slot = place + lax.rem(peer, 2) * (n - 1 - 2 * place)
        return pltpu.make_async_remote_copy(
            src_ref=anoms_ref.at[peer], dst_ref=buf.at[slot, tile], send_sem=a_send.at[k],
            recv_sem=a_recv.at[k], device_id=(peer, place), device_id_type=MESH)

    def moved(j, c, to):
        return pltpu.make_async_remote_copy(
            src_ref=buf.at[j, c], dst_ref=buf.at[j, c], send_sem=z_send.at[j, c],
            recv_sem=z_recv.at[j, c], device_id=(tile, mirrored(to)), device_id_type=MESH)

    def side_moved(j, to, which):
        ref = slots[which]
        return pltpu.make_async_remote_copy(
            src_ref=ref.at[j], dst_ref=ref.at[j], send_sem=s_send.at[j, which],
            recv_sem=s_recv.at[j, which], device_id=(tile, mirrored(to)), device_id_type=MESH)

    def given(j, source):
        return pltpu.make_async_remote_copy(
            src_ref=gave.at[j], dst_ref=got.at[source], send_sem=g_send.at[j],
            recv_sem=g_recv.at[source], device_id=(tile, mirrored(j)), device_id_type=MESH)

    sends_right = u < half
    sends_left = u > half
    sends_own = u != half
    own_to = jnp.where(u < half, u + 1, jnp.maximum(u - 1, 0))

    if exchange:
        for k in range(1, tiles):
            exchanged(k).start()
        here = [pltpu.make_async_copy(anoms_ref.at[tile], buf.at[u, tile], local.at[0])]
    else:
        here = [pltpu.make_async_copy(anoms_ref, buf.at[u], local.at[0])]
    for i in range(5):
        here.append(pltpu.make_async_copy(small_refs[i], slots[i].at[u], local.at[i + 1]))
    for copy in here:
        copy.start()
    for copy in here:
        copy.wait()

    def small_start(j, to):
        for i in range(5):
            side_moved(j, to, i).start()

    @pl.when(sends_right)
    def _():
        small_start(u, own_to)

    def piece_at(k):
        return lax.rem(tile + pieces - k, pieces) if exchange else k

    for k in range(pieces):
        if exchange and k > 0:
            exchanged(k).wait_recv()

        @pl.when(sends_right)
        def _():
            moved(u, piece_at(k), own_to).start()

    def hot_of(j, ref):
        row = maps[j]
        for c in range(0, rows, BLOCK):
            at = lax.broadcasted_iota(jnp.int32, (BLOCK, rows), 0) + c
            ref[c:c + BLOCK, :] = jnp.where(at == row, 1.0, 0.0).astype(BF16)

    def link_parts(j):
        links = patterns[j].astype(F32) * scales[j] / (members - 1)
        if blocks % 8:
            links = jnp.concatenate([links, jnp.zeros((8 - blocks, n * blocks), F32)], axis=0)
        return jnp.concatenate(parts(links), axis=0).astype(BF16)

    def prepare(j, hot, back):
        where = positions[j].astype(F32)
        vecs = vectors[j].astype(F32)
        side = stacked([where[0:1], where[1:2], where[2:3]], rows, 8)
        columns = n * blocks
        block_of = lax.broadcasted_iota(jnp.int32, (columns, rows), 1) // BLOCK
        at = lax.broadcasted_iota(jnp.int32, (columns, rows), 0)
        spread = jnp.where(at == block_of + mirrored(j) * blocks, 1.0, 0.0).astype(BF16)
        w = dot(link_parts(u), spread, NN)
        w = w[0:8] + w[8:16] + w[16:24]
        values = list(parts(vecs[0:1] * w)) + list(parts(vecs[1:2] * w)) + [side]
        if back:
            take = jnp.where(
                lax.broadcasted_iota(jnp.int32, (columns, 8), 0)
                == lax.broadcasted_iota(jnp.int32, (columns, 8), 1) + place * blocks, 1.0, 0.0).astype(BF16)
            taken = dot(link_parts(j), take, NN)
            repeated = jnp.where(
                lax.broadcasted_iota(jnp.int32, (8, rows), 1) // BLOCK
                == lax.broadcasted_iota(jnp.int32, (8, rows), 0), 1.0, 0.0)
            for i in range(3):
                values.append(dot(taken[8 * i:8 * i + 8].astype(BF16), repeated.astype(BF16), TN))
        if len(values) % 2:
            values.append(jnp.zeros((8, rows), F32))
        turned = dot(jnp.concatenate(values, axis=0).astype(BF16), hot[...], NT)
        lines = [turned[0:8] + turned[8:16] + turned[16:24], turned[24:32] + turned[32:40] + turned[40:48]]
        if back:
            lines.append(turned[56:64] + turned[64:72] + turned[72:80])
        for b in range(blocks):
            for i, line in enumerate(lines):
                w_row[b, i:i + 1, :] = line[b:b + 1]
        x, y, z = turned[48:49], turned[49:50], turned[50:51]
        q_aug[...] = stacked(
            [-2.0 * x, -2.0 * y, -2.0 * z, 1.0, 1.0, 1.0, *parts(squared_length(x, y, z))],
            rows).astype(BF16)

    from_left = jnp.minimum(u, half)

    def arrive_small(j, onward, to):
        @pl.when(j >= 0)
        def _():
            for i in range(5):
                side_moved(j, to, i).wait_recv()

            @pl.when(onward)
            def _():
                small_start(j, to)

    def arrive_piece(j, c, onward, to):
        moved(j, c, to).wait_recv()

        @pl.when(onward)
        def _():
            moved(j, c, to).start()

    chunk = 2 * BLOCK
    per_chunk = rows // chunk

    def pair(j, back, following):
        if back:
            gave[j] = jnp.zeros((8, rows), F32)

        onward, to = u < n - 1, jnp.minimum(u + 1, n - 1)
        arrive_small(following, onward, to)

        def one(b, carry):
            first, last = lax.div(b * pieces, blocks), lax.div((b + 1) * pieces, blocks)
            for i in range(-(-pieces // blocks)):
                @pl.when((following >= 0) & (first + i < last))
                def _():
                    arrive_piece(following, piece_at(first + i), onward, to)

            start = pl.multiple_of(b * BLOCK, BLOCK)
            mine = own[pl.ds(start, BLOCK), :]
            mine_aug = p_aug[:, pl.ds(start, BLOCK)]
            theirs = buf[j].reshape(rows, members)
            sums = [jnp.zeros((BLOCK, BLOCK), F32)] * 2
            for c in range(per_chunk):
                cut = slice(c * chunk, (c + 1) * chunk)
                cov = dot(mine, theirs[cut], NT)
                kern = cov * gaspari_cohn(dot(mine_aug, q_aug[:, cut], TN))
                for v in range(2):
                    term = kern * w_row[b, v:v + 1, cut]
                    sums[v] = sums[v] + term[:, :BLOCK] + term[:, BLOCK:]
                    if back:
                        column = v_col[v, pl.ds(start, BLOCK), :]
                        for s in range(2):
                            lanes = slice(c * chunk + s * BLOCK, c * chunk + (s + 1) * BLOCK)
                            down = jnp.sum(kern[:, s * BLOCK:(s + 1) * BLOCK] * column, axis=0, keepdims=True)
                            gave[j, v:v + 1, lanes] += down * w_row[b, 2:3, lanes]
            for v in range(2):
                acc[v, pl.ds(start, BLOCK), :] += sums[v]
            return carry

        lax.fori_loop(0, blocks, one, 0)

    acc[...] = jnp.zeros_like(acc)
    hot_of(u, own_hot)
    own[...] = dot(own_hot[...], buf[u].reshape(rows, members), TN).astype(BF16)
    where = positions[u].astype(F32)
    x, y, z = where[0:1], where[1:2], where[2:3]
    p_aug[...] = stacked(
        [x, y, z, *parts(squared_length(x, y, z)), 1.0, 1.0, 1.0], rows).astype(BF16)
    vecs = vectors[u].astype(F32)
    both = stacked([vecs[0:1], vecs[1:2]], rows).astype(BF16)
    for v in range(2):
        pick = jnp.where(lax.broadcasted_iota(jnp.int32, (16, BLOCK), 0) == v, 1.0, 0.0).astype(BF16)
        v_col[v] = dot(both, pick, TN)
    prepare(u, own_hot, False)
    pair(u, False, from_left - 1)

    @pl.when(sends_left)
    def _():
        small_start(u, own_to)
        for k in range(pieces):
            moved(u, piece_at(k), own_to).start()

    def work(j, following):
        hot_of(j, one_hot)
        prepare(j, one_hot, True)
        pair(j, True, following)
        given(j, u).start()

    def distance(d, carry):
        right = from_left - d
        left = u + d

        @pl.when(right >= 0)
        def _():
            work(right, right - 1)

        @pl.when((u >= half) & (left < n))
        def _():
            onward, to = u > half, jnp.maximum(u - 1, 0)
            arrive_small(left, onward, to)
            for k in range(pieces):
                arrive_piece(left, piece_at(k), onward, to)
            work(left, -1)

        return carry

    lax.fori_loop(1, max(half, n - 1 - half) + 1, distance, 0)

    total = jnp.zeros((8, rows), F32)
    got_any = []
    for other in range(n):
        comes = ((u < half) & (other > u)) | ((u > half) & (other >= half) & (other < u))

        @pl.when(comes)
        def _():
            given(other, other).wait_recv()

        @pl.when(jnp.logical_not(comes))
        def _():
            got[other] = jnp.zeros((8, rows), F32)

        total = total + got[other]
    returned = jnp.concatenate([*parts(total), jnp.zeros((8, rows), F32)], axis=0).astype(BF16)
    turned = dot(returned, own_hot[...], NN)
    out = turned[0:8] + turned[8:16] + turned[16:24]
    ones = jnp.ones((8, BLOCK), F32)
    for v in range(2):
        line = lax.dot_general(ones, acc[v], NT, precision=lax.Precision.HIGHEST, preferred_element_type=F32)
        out_ref[v:v + 1, :] = out[v:v + 1] + line[0:1]

    if exchange:
        for k in range(1, tiles):
            exchanged(k).wait_send()
    for j in range(n):
        passes = ((j == u) & sends_own) | ((j < from_left) & (u < n - 1)) | ((j > u) & (u > half))

        @pl.when(passes)
        def _():
            for i in range(5):
                side_moved(j, own_to, i).wait_send()
            for c in range(pieces):
                moved(j, c, own_to).wait_send()

        @pl.when((j < from_left) | ((j > u) & (u >= half)))
        def _():
            given(j, u).wait_send()


def on_device(n, tiles, model_anoms, block_map, vectors, positions, pattern, pair_scale):
    rows, members = model_anoms.shape
    blocks = rows // BLOCK
    exchange = rows % (16 * tiles) == 0
    if exchange:
        pieces = tiles
        anoms = model_anoms.reshape(pieces, rows // pieces, members)
    else:
        pieces = rows // BLOCK
        anoms = lax.all_to_all(model_anoms, "tile", split_axis=0, concat_axis=0, tiled=True)
        anoms = anoms.reshape(pieces, rows // pieces, members)
    vmem = pl.BlockSpec(memory_space=pltpu.VMEM)
    dma = pltpu.SemaphoreType.DMA
    return pl.pallas_call(
        functools.partial(kernel, n, tiles, blocks, exchange),
        out_shape=jax.ShapeDtypeStruct((2, rows), F32),
        in_specs=[vmem] * 6,
        out_specs=vmem,
        scratch_shapes=[
            pltpu.VMEM((n, pieces, rows // pieces, members), BF16),
            pltpu.VMEM((n, 3, rows), BF16),
            pltpu.VMEM((n, 2, rows), BF16),
            pltpu.VMEM((n, 1, rows), jnp.int32),
            pltpu.VMEM((n, blocks, n * blocks), jnp.int32),
            pltpu.VMEM((n, blocks, n * blocks), F32),
            pltpu.VMEM((rows, rows), BF16),
            pltpu.VMEM((rows, rows), BF16),
            pltpu.VMEM((rows, members), BF16),
            pltpu.VMEM((16, rows), BF16),
            pltpu.VMEM((16, rows), BF16),
            pltpu.VMEM((2, rows, BLOCK), F32),
            pltpu.VMEM((blocks, 8, rows), F32),
            pltpu.VMEM((2, rows, BLOCK), F32),
            pltpu.VMEM((n, 8, rows), F32),
            pltpu.VMEM((n, 8, rows), F32),
            dma((tiles,)), dma((tiles,)),
            dma((n, pieces)), dma((n, pieces)),
            dma((n, 5)), dma((n, 5)),
            dma((n,)), dma((n,)),
            dma((6,)),
        ],
        compiler_params=pltpu.CompilerParams(
            collective_id=0, has_side_effects=True, vmem_limit_bytes=56 * 2**20),
    )(anoms, positions, vectors, block_map, pattern, pair_scale)


def solution(mesh):
    shape = dict(mesh.shape)
    return jax.shard_map(
        functools.partial(on_device, shape["blk"], shape["tile"]),
        mesh=mesh,
        in_specs=(
            P(("tile", "blk"), None),
            P(("tile", "blk"), None),
            P(None, ("tile", "blk")),
            P(None, ("tile", "blk")),
            P(("tile", "blk"), None),
            P(("tile", "blk"), None),
        ),
        out_specs=P(None, ("tile", "blk")),
        check_vma=False,
    )
```

```python
import functools

import jax
import jax.numpy as jnp
from jax import lax
from jax.experimental import pallas as pl
from jax.experimental.pallas import tpu as pltpu
from jax.sharding import PartitionSpec as P

BLOCK = 128
F32, BF16 = jnp.float32, jnp.bfloat16
MESH = pl.DeviceIdType.MESH
NT = (((1,), (1,)), ((), ()))
TN = (((0,), (0,)), ((), ()))
NN = (((1,), (0,)), ((), ()))


def dot(a, b, dims):
    return lax.dot_general(a, b, dims, preferred_element_type=F32)


def parts(x):
    high = x.astype(BF16).astype(F32)
    rest = x - high
    mid = rest.astype(BF16).astype(F32)
    return high, mid, rest - mid


def stacked(rows, width, height=16):
    at = lax.broadcasted_iota(jnp.int32, (height, width), 0)
    out = jnp.zeros((height, width), F32)
    for i, row in enumerate(rows):
        out = jnp.where(at == i, row, out)
    return out


def squared_length(x, y, z):
    return x * x + y * y + z * z


def gaspari_cohn(squared):
    squared = jnp.maximum(squared, 1e-20)
    inverse = lax.rsqrt(squared)
    r = squared * inverse
    t = jnp.maximum(2.0 - r, 0.0)
    t = t * t
    outer = (t * t) * (r * (1.0 / 12.0) + (1.0 / 6.0) - inverse * (1.0 / 24.0))
    inner = (((-0.25 * r + 0.5) * r + 0.625) * r - 5.0 / 3.0) * squared + 1.0
    return jnp.where(squared <= 1.0, inner, outer)


def kernel(n, tiles, blocks, exchange, anoms_ref, *refs):
    small_refs, (out_ref, buf), slots = refs[:5], refs[5:7], refs[7:12]
    (one_hot, own_hot, own, p_aug, q_aug, v_col, w_row, acc,
     gave, got, a_send, a_recv, z_send, z_recv, s_send, s_recv, g_send, g_recv, local) = refs[12:]
    positions, vectors, maps, patterns, scales = slots
    tile, place = lax.axis_index("tile"), lax.axis_index("blk")
    half = n // 2
    pieces, piece, members = buf.shape[1:]
    rows = pieces * piece
    flip = lax.rem(tile, 2)

    def mirrored(i):
        return i + flip * (n - 1 - 2 * i)

    u = mirrored(place)

    barrier = pltpu.get_barrier_semaphore()
    greeted = n - 1
    for k in range(1, n):
        pl.semaphore_signal(barrier, inc=1, device_id=(tile, lax.rem(place + k, n)), device_id_type=MESH)
    if exchange:
        greeted += tiles - 1
        for k in range(1, tiles):
            pl.semaphore_signal(barrier, inc=1, device_id=(lax.rem(tile + k, tiles), place), device_id_type=MESH)
    pl.semaphore_wait(barrier, greeted)

    def exchanged(k):
        peer = lax.rem(tile + k, tiles)
        slot = place + lax.rem(peer, 2) * (n - 1 - 2 * place)
        return pltpu.make_async_remote_copy(
            src_ref=anoms_ref.at[peer], dst_ref=buf.at[slot, tile], send_sem=a_send.at[k],
            recv_sem=a_recv.at[k], device_id=(peer, place), device_id_type=MESH)

    def moved(j, c, to):
        return pltpu.make_async_remote_copy(
            src_ref=buf.at[j, c], dst_ref=buf.at[j, c], send_sem=z_send.at[j, c],
            recv_sem=z_recv.at[j, c], device_id=(tile, mirrored(to)), device_id_type=MESH)

    def side_moved(j, to, which):
        ref = slots[which]
        return pltpu.make_async_remote_copy(
            src_ref=ref.at[j], dst_ref=ref.at[j], send_sem=s_send.at[j, which],
            recv_sem=s_recv.at[j, which], device_id=(tile, mirrored(to)), device_id_type=MESH)

    def given(j, source):
        return pltpu.make_async_remote_copy(
            src_ref=gave.at[j], dst_ref=got.at[source], send_sem=g_send.at[j],
            recv_sem=g_recv.at[source], device_id=(tile, mirrored(j)), device_id_type=MESH)

    sends_right = u < half
    sends_left = u > half
    sends_own = u != half
    own_to = jnp.where(u < half, u + 1, jnp.maximum(u - 1, 0))

    if exchange:
        for k in range(1, tiles):
            exchanged(k).start()
        here = [pltpu.make_async_copy(anoms_ref.at[tile], buf.at[u, tile], local.at[0])]
    else:
        here = [pltpu.make_async_copy(anoms_ref, buf.at[u], local.at[0])]
    for i in range(5):
        here.append(pltpu.make_async_copy(small_refs[i], slots[i].at[u], local.at[i + 1]))
    for copy in here:
        copy.start()
    for copy in here:
        copy.wait()

    def small_start(j, to):
        for i in range(5):
            side_moved(j, to, i).start()

    @pl.when(sends_right)
    def _():
        small_start(u, own_to)

    def piece_at(k):
        return lax.rem(tile + pieces - k, pieces) if exchange else k

    for k in range(pieces):
        if exchange and k > 0:
            exchanged(k).wait_recv()

        @pl.when(sends_right)
        def _():
            moved(u, piece_at(k), own_to).start()

    def hot_of(j, ref):
        row = maps[j]
        for c in range(0, rows, BLOCK):
            at = lax.broadcasted_iota(jnp.int32, (BLOCK, rows), 0) + c
            ref[c:c + BLOCK, :] = jnp.where(at == row, 1.0, 0.0).astype(BF16)

    def link_parts(j):
        links = patterns[j].astype(F32) * scales[j] / (members - 1)
        if blocks % 8:
            links = jnp.concatenate([links, jnp.zeros((8 - blocks, n * blocks), F32)], axis=0)
        return jnp.concatenate(parts(links), axis=0).astype(BF16)

    def prepare(j, hot, back):
        where = positions[j].astype(F32)
        vecs = vectors[j].astype(F32)
        side = stacked([where[0:1], where[1:2], where[2:3]], rows, 8)
        columns = n * blocks
        block_of = lax.broadcasted_iota(jnp.int32, (columns, rows), 1) // BLOCK
        at = lax.broadcasted_iota(jnp.int32, (columns, rows), 0)
        spread = jnp.where(at == block_of + mirrored(j) * blocks, 1.0, 0.0).astype(BF16)
        w = dot(link_parts(u), spread, NN)
        w = w[0:8] + w[8:16] + w[16:24]
        values = list(parts(vecs[0:1] * w)) + list(parts(vecs[1:2] * w)) + [side]
        if back:
            take = jnp.where(
                lax.broadcasted_iota(jnp.int32, (columns, 8), 0)
                == lax.broadcasted_iota(jnp.int32, (columns, 8), 1) + place * blocks, 1.0, 0.0).astype(BF16)
            taken = dot(link_parts(j), take, NN)
            repeated = jnp.where(
                lax.broadcasted_iota(jnp.int32, (8, rows), 1) // BLOCK
                == lax.broadcasted_iota(jnp.int32, (8, rows), 0), 1.0, 0.0)
            for i in range(3):
                values.append(dot(taken[8 * i:8 * i + 8].astype(BF16), repeated.astype(BF16), TN))
        if len(values) % 2:
            values.append(jnp.zeros((8, rows), F32))
        turned = dot(jnp.concatenate(values, axis=0).astype(BF16), hot[...], NT)
        lines = [turned[0:8] + turned[8:16] + turned[16:24], turned[24:32] + turned[32:40] + turned[40:48]]
        if back:
            lines.append(turned[56:64] + turned[64:72] + turned[72:80])
        for b in range(blocks):
            for i, line in enumerate(lines):
                w_row[b, i:i + 1, :] = line[b:b + 1]
        x, y, z = turned[48:49], turned[49:50], turned[50:51]
        q_aug[...] = stacked(
            [-2.0 * x, -2.0 * y, -2.0 * z, 1.0, 1.0, 1.0, *parts(squared_length(x, y, z))],
            rows).astype(BF16)

    from_left = jnp.minimum(u, half)

    def arrive_small(j, onward, to):
        @pl.when(j >= 0)
        def _():
            for i in range(5):
                side_moved(j, to, i).wait_recv()

            @pl.when(onward)
            def _():
                small_start(j, to)

    def arrive_piece(j, c, onward, to):
        moved(j, c, to).wait_recv()

        @pl.when(onward)
        def _():
            moved(j, c, to).start()

    chunk = 2 * BLOCK
    per_chunk = rows // chunk

    def pair(j, back, following):
        if back:
            gave[j] = jnp.zeros((8, rows), F32)

        onward, to = u < n - 1, jnp.minimum(u + 1, n - 1)
        arrive_small(following, onward, to)

        def one(b, carry):
            first, last = lax.div(b * pieces, blocks), lax.div((b + 1) * pieces, blocks)
            for i in range(-(-pieces // blocks)):
                @pl.when((following >= 0) & onward & (first + i < last))
                def _():
                    arrive_piece(following, piece_at(first + i), onward, to)

            start = pl.multiple_of(b * BLOCK, BLOCK)
            mine = own[pl.ds(start, BLOCK), :]
            mine_aug = p_aug[:, pl.ds(start, BLOCK)]
            theirs = buf[j].reshape(rows, members)
            sums = [jnp.zeros((BLOCK, BLOCK), F32)] * 2
            for c in range(per_chunk):
                cut = slice(c * chunk, (c + 1) * chunk)
                cov = dot(mine, theirs[cut], NT)
                kern = cov * gaspari_cohn(dot(mine_aug, q_aug[:, cut], TN))
                for v in range(2):
                    term = kern * w_row[b, v:v + 1, cut]
                    sums[v] = sums[v] + term[:, :BLOCK] + term[:, BLOCK:]
                    if back:
                        column = v_col[v, pl.ds(start, BLOCK), :]
                        for s in range(2):
                            lanes = slice(c * chunk + s * BLOCK, c * chunk + (s + 1) * BLOCK)
                            down = jnp.sum(kern[:, s * BLOCK:(s + 1) * BLOCK] * column, axis=0, keepdims=True)
                            gave[j, v:v + 1, lanes] += down * w_row[b, 2:3, lanes]
            for v in range(2):
                acc[v, pl.ds(start, BLOCK), :] += sums[v]
            return carry

        lax.fori_loop(0, blocks, one, 0)

    acc[...] = jnp.zeros_like(acc)
    hot_of(u, own_hot)
    own[...] = dot(own_hot[...], buf[u].reshape(rows, members), TN).astype(BF16)
    where = positions[u].astype(F32)
    x, y, z = where[0:1], where[1:2], where[2:3]
    p_aug[...] = stacked(
        [x, y, z, *parts(squared_length(x, y, z)), 1.0, 1.0, 1.0], rows).astype(BF16)
    vecs = vectors[u].astype(F32)
    both = stacked([vecs[0:1], vecs[1:2]], rows).astype(BF16)
    for v in range(2):
        pick = jnp.where(lax.broadcasted_iota(jnp.int32, (16, BLOCK), 0) == v, 1.0, 0.0).astype(BF16)
        v_col[v] = dot(both, pick, TN)
    @pl.when(sends_left)
    def _():
        small_start(u, own_to)
        for k in range(pieces):
            moved(u, piece_at(k), own_to).start()

    prepare(u, own_hot, False)
    pair(u, False, from_left - 1)

    def work(j, following):
        @pl.when((u == n - 1) & (j < half))
        def _():
            for k in range(pieces):
                arrive_piece(j, piece_at(k), False, 0)

        hot_of(j, one_hot)
        prepare(j, one_hot, True)
        pair(j, True, following)
        given(j, u).start()

    def distance(d, carry):
        right = from_left - d
        left = u + d

        @pl.when(right >= 0)
        def _():
            work(right, right - 1)

        @pl.when((u >= half) & (left < n))
        def _():
            onward, to = u > half, jnp.maximum(u - 1, 0)
            arrive_small(left, onward, to)
            for k in range(pieces):
                arrive_piece(left, piece_at(k), onward, to)
            work(left, -1)

        return carry

    lax.fori_loop(1, max(half, n - 1 - half) + 1, distance, 0)

    total = jnp.zeros((8, rows), F32)
    got_any = []
    for other in range(n):
        comes = ((u < half) & (other > u)) | ((u > half) & (other >= half) & (other < u))

        @pl.when(comes)
        def _():
            given(other, other).wait_recv()

        @pl.when(jnp.logical_not(comes))
        def _():
            got[other] = jnp.zeros((8, rows), F32)

        total = total + got[other]
    returned = jnp.concatenate([*parts(total), jnp.zeros((8, rows), F32)], axis=0).astype(BF16)
    turned = dot(returned, own_hot[...], NN)
    out = turned[0:8] + turned[8:16] + turned[16:24]
    ones = jnp.ones((8, BLOCK), F32)
    for v in range(2):
        line = lax.dot_general(ones, acc[v], NT, precision=lax.Precision.HIGHEST, preferred_element_type=F32)
        out_ref[v:v + 1, :] = out[v:v + 1] + line[0:1]

    if exchange:
        for k in range(1, tiles):
            exchanged(k).wait_send()
    for j in range(n):
        passes = ((j == u) & sends_own) | ((j < from_left) & (u < n - 1)) | ((j > u) & (u > half))

        @pl.when(passes)
        def _():
            for i in range(5):
                side_moved(j, own_to, i).wait_send()
            for c in range(pieces):
                moved(j, c, own_to).wait_send()

        @pl.when((j < from_left) | ((j > u) & (u >= half)))
        def _():
            given(j, u).wait_send()


def on_device(n, tiles, model_anoms, block_map, vectors, positions, pattern, pair_scale):
    rows, members = model_anoms.shape
    blocks = rows // BLOCK
    exchange = rows % (16 * tiles) == 0
    if exchange:
        pieces = tiles
        anoms = model_anoms.reshape(pieces, rows // pieces, members)
    else:
        pieces = rows // BLOCK
        anoms = lax.all_to_all(model_anoms, "tile", split_axis=0, concat_axis=0, tiled=True)
        anoms = anoms.reshape(pieces, rows // pieces, members)
    vmem = pl.BlockSpec(memory_space=pltpu.VMEM)
    dma = pltpu.SemaphoreType.DMA
    return pl.pallas_call(
        functools.partial(kernel, n, tiles, blocks, exchange),
        out_shape=jax.ShapeDtypeStruct((2, rows), F32),
        in_specs=[vmem] * 6,
        out_specs=vmem,
        scratch_shapes=[
            pltpu.VMEM((n, pieces, rows // pieces, members), BF16),
            pltpu.VMEM((n, 3, rows), BF16),
            pltpu.VMEM((n, 2, rows), BF16),
            pltpu.VMEM((n, 1, rows), jnp.int32),
            pltpu.VMEM((n, blocks, n * blocks), jnp.int32),
            pltpu.VMEM((n, blocks, n * blocks), F32),
            pltpu.VMEM((rows, rows), BF16),
            pltpu.VMEM((rows, rows), BF16),
            pltpu.VMEM((rows, members), BF16),
            pltpu.VMEM((16, rows), BF16),
            pltpu.VMEM((16, rows), BF16),
            pltpu.VMEM((2, rows, BLOCK), F32),
            pltpu.VMEM((blocks, 8, rows), F32),
            pltpu.VMEM((2, rows, BLOCK), F32),
            pltpu.VMEM((n, 8, rows), F32),
            pltpu.VMEM((n, 8, rows), F32),
            dma((tiles,)), dma((tiles,)),
            dma((n, pieces)), dma((n, pieces)),
            dma((n, 5)), dma((n, 5)),
            dma((n,)), dma((n,)),
            dma((6,)),
        ],
        compiler_params=pltpu.CompilerParams(
            collective_id=0, has_side_effects=True, vmem_limit_bytes=56 * 2**20),
    )(anoms, positions, vectors, block_map, pattern, pair_scale)


def solution(mesh):
    shape = dict(mesh.shape)
    return jax.shard_map(
        functools.partial(on_device, shape["blk"], shape["tile"]),
        mesh=mesh,
        in_specs=(
            P(("tile", "blk"), None),
            P(("tile", "blk"), None),
            P(None, ("tile", "blk")),
            P(None, ("tile", "blk")),
            P(("tile", "blk"), None),
            P(("tile", "blk"), None),
        ),
        out_specs=P(None, ("tile", "blk")),
        check_vma=False,
    )
```
